32 devices in a mesh: tile: 8 (over z, y), grp: 4 (over x, core).
Axes of the slice: x: 2, y: 2, z: 4, core: 2. Of those that a mesh axis runs over, the one named last changes fastest.
Arguments:
- left_triples: bfloat16 [256, 6144, 300], P('tile', 'grp'), may hold values from -6 to 6
- right_triples: bfloat16 [256, 6144, 300], P('tile', 'grp'), may hold values from -6 to 6
- live_tiles: int32 [256, 24], P('tile', 'grp'), may hold values from 0 to 1
- vv_block: bfloat16 [300, 300], replicated, may hold values from -0.375 to 0.375
- slab_block: bfloat16 [256, 256], replicated, may hold values from -0.375 to 0.375
- left_doubles: bfloat16 [256, 8192], P('tile', 'grp'), may hold values from -6 to 6
- ov_block: bfloat16 [30, 300], replicated, may hold values from -6 to 6
- pair_index: int32 [6144], P('grp'), may hold values from 0 to 8191
- occ_index: int32 [6144], P('grp'), may hold values from 0 to 29
Outputs:
- sigma_out: bfloat16 [256, 6144, 300], P('tile', 'grp')
- density: float32 [300, 300], replicated
The draws below stay inside these ranges and needn't reach their ends.
All inputs are finite; a program needn't handle non-finite values.
Results may differ from the reference program's by a relative error of at most 0.0026.
Values may be sent and summed in bfloat16 or wider, within the bound.
No kernel may reach another device: no remote copies, remote signals or barrier semaphores. Data moves between devices by JAX's collectives and lax.ppermute only.
A program may use at most 320 MiB of HBM per device.

```python
import math
import jax
import jax.numpy as jnp
from jax import lax

NOCC = 30
NVIR = 300
NSLAB = 256
TILE_ROWS = 256
NPAIR = 8192
ROWS = 6144
NTILES = 24


def draw_live_tiles(key, part):
    first_key, second_key = jax.random.split(jax.random.fold_in(key, 11))
    level = jax.random.randint(first_key, (NSLAB, 1), 0, 5)
    chance = jnp.array([6, 12, 24, 48, 96], jnp.int32)[level]
    rolled = jax.random.randint(second_key, (NSLAB, NTILES), 0, 100)
    return (rolled < chance).astype(jnp.int32)


def with_ends(values, own_key, least, high):
    longest = values.shape.index(max(values.shape))
    spots = []
    for shift in (0, 1):
        where = [jax.random.randint(jax.random.fold_in(own_key, axis), (), 0, length) for axis, length in enumerate(values.shape)]
        where[longest] = (where[longest] + shift) % values.shape[longest]
        spots.append(tuple(where))
    return values.at[spots[0]].set(least).at[spots[1]].set(high)


def level_of(rng, shape, cuts, smallest, high):
    loudness, own = 1.0, jax.random.fold_in(rng, 6)
    for axis_at, parts in cuts:
        heights = jnp.exp(jax.random.uniform(jax.random.fold_in(own, axis_at), (parts,), jnp.float32, smallest / len(cuts), high / len(cuts)))
        loudness = loudness * jnp.repeat(heights, shape[axis_at] // parts).reshape([-1 if axis == axis_at else 1 for axis in range(len(shape))])
    return loudness


def bell_draw(rng, dims, spread, limit, shards=(), kind=jnp.bfloat16):
    gain = level_of(rng, dims, shards, -0.22, 0.18) if shards else 1.0
    values = jax.random.normal(rng, dims, jnp.float32) * spread * gain
    return jnp.minimum(jnp.maximum(values, -limit), limit).astype(kind)


def setup_inputs(seed: int = 0) -> dict:
    streams_of = jax.random.split(jax.random.key(seed), 10)
    left_triples = bell_draw(streams_of[0], (NSLAB, ROWS, NVIR), 1.0, 6.0, ((0, 8), (1, 4)))
    right_triples = bell_draw(streams_of[1], (NSLAB, ROWS, NVIR), 1.0, 6.0, ((0, 8), (1, 4)))
    live_tiles = draw_live_tiles(jax.random.fold_in(streams_of[9], 71), 0)
    vv_block = bell_draw(streams_of[3], (NVIR, NVIR), NVIR ** -0.5, 0.375)
    slab_block = bell_draw(streams_of[4], (NSLAB, NSLAB), NSLAB ** -0.5, 0.375)
    left_doubles = bell_draw(streams_of[5], (NSLAB, NPAIR), 1.0, 6.0, ((0, 8), (1, 4)))
    ov_block = bell_draw(streams_of[6], (NOCC, NVIR), 1.0, 6.0)
    pair_index = with_ends(jax.random.randint(streams_of[7], (ROWS,), 0, NPAIR), jax.random.fold_in(streams_of[7], 1), 0, NPAIR - 1).astype(jnp.int32)
    occ_index = with_ends(jax.random.randint(streams_of[8], (ROWS,), 0, NOCC), jax.random.fold_in(streams_of[8], 1), 0, NOCC - 1).astype(jnp.int32)
    return {"left_triples": left_triples, "right_triples": right_triples, "live_tiles": live_tiles, "vv_block": vv_block, "slab_block": slab_block, "left_doubles": left_doubles, "ov_block": ov_block, "pair_index": pair_index, "occ_index": occ_index}


def reference(left_triples, right_triples, live_tiles, vv_block, slab_block, left_doubles, ov_block, pair_index, occ_index):
    live_mask = live_tiles.astype(jnp.float32)
    occ_rows = ov_block[occ_index].astype(jnp.float32)
    picked = left_doubles[:, pair_index].astype(jnp.float32)

    def advance(running, tile_pos):
        offset = (tile_pos * TILE_ROWS).astype(jnp.int32)
        left_part = lax.dynamic_slice_in_dim(left_triples, offset, TILE_ROWS, 1)
        right_part = lax.dynamic_slice_in_dim(right_triples, offset, TILE_ROWS, 1)
        flags = lax.dynamic_slice_in_dim(live_mask, tile_pos.astype(jnp.int32), 1, 1)
        masked = (left_part.astype(jnp.float32) * flags[:, :, None]).astype(jnp.bfloat16)
        flat_rows = masked.reshape(-1, NVIR)
        vv_term = jnp.dot(flat_rows, vv_block, preferred_element_type=jnp.float32).reshape(NSLAB, TILE_ROWS, NVIR)
        slab_term = jnp.einsum('bd,drc->brc', slab_block.astype(jnp.float32), masked.astype(jnp.float32)).astype(jnp.bfloat16)
        pair_part = lax.dynamic_slice_in_dim(picked, offset, TILE_ROWS, 1)
        occ_part = lax.dynamic_slice_in_dim(occ_rows, offset, TILE_ROWS, 0)
        pair_term = pair_part[:, :, None] * occ_part[None, :, :]
        summed = (vv_term + slab_term.astype(jnp.float32) + pair_term) * flags[:, :, None]
        running = running + lax.dot_general(flat_rows, right_part.reshape(-1, NVIR), (((0,), (0,)), ((), ())), preferred_element_type=jnp.float32)
        return (running, summed.astype(jnp.bfloat16))
    density, pieces = lax.scan(advance, jnp.zeros((NVIR, NVIR), jnp.float32), jnp.arange(NTILES, dtype=jnp.int32))
    sigma_out = jnp.moveaxis(pieces, 0, 1).reshape(NSLAB, ROWS, NVIR)
    return (sigma_out, density / math.sqrt(NSLAB * ROWS))
```

```python
import functools
import math

import jax
import jax.numpy as jnp
from jax import lax
from jax.experimental import pallas as pl
from jax.experimental.pallas import tpu as pltpu
from jax.sharding import PartitionSpec as P

LANES = 128
VMEM_BYTES = 56 << 20


def plain_body(
    left_triples,
    right_triples,
    live_tiles,
    vv_block,
    slab_block,
    left_doubles,
    ov_block,
    pair_index,
    occ_index,
):
    slab_count, row_count, feature = left_triples.shape
    tile_count = live_tiles.shape[1]
    tile_rows = row_count // tile_count
    live_mask = live_tiles.astype(jnp.bfloat16)
    masked = (
        left_triples.reshape(slab_count, tile_count, tile_rows, feature)
        * live_mask[:, :, None, None]
    ).reshape(slab_count, row_count, feature)
    mixed_rows = jnp.einsum(
        "bd,drc->brc",
        slab_block,
        lax.all_to_all(masked, "tile", split_axis=1, concat_axis=0, tiled=True),
        preferred_element_type=jnp.float32,
    ).astype(jnp.bfloat16)
    slab_term = lax.all_to_all(mixed_rows, "tile", split_axis=0, concat_axis=1, tiled=True)
    full_table = lax.all_gather(left_doubles, "grp", axis=1, tiled=True)
    picked = jnp.take(full_table, pair_index, axis=1).astype(jnp.float32)
    onehot = (occ_index[:, None] == jnp.arange(ov_block.shape[0], dtype=jnp.int32)[None, :]).astype(
        jnp.bfloat16
    )
    occ_rows = jnp.dot(onehot, ov_block, preferred_element_type=jnp.float32)
    pair_term = picked[:, :, None] * occ_rows[None, :, :]
    flat_rows = masked.reshape(-1, feature)
    vv_term = jnp.dot(flat_rows, vv_block, preferred_element_type=jnp.float32).reshape(
        slab_count, row_count, feature
    )
    partial_value = lax.dot_general(
        flat_rows,
        right_triples.reshape(-1, feature),
        (((0,), (0,)), ((), ())),
        preferred_element_type=jnp.float32,
    )
    summed = vv_term + slab_term.astype(jnp.float32) + pair_term
    summed = (
        summed.reshape(slab_count, tile_count, tile_rows, feature)
        * live_tiles.astype(jnp.float32)[:, :, None, None]
    )
    sigma_out = summed.reshape(slab_count, row_count, feature).astype(jnp.bfloat16)
    norm_scale = math.sqrt(slab_count * lax.axis_size("tile") * row_count * lax.axis_size("grp"))
    density = lax.psum(partial_value, ("tile", "grp")) / norm_scale
    return (sigma_out, density)


def pack_kernel(tiles, place_ref, left_ref, out_ref):
    cap = out_ref.shape[2]
    units = left_ref.shape[0]
    span = left_ref.shape[2] // tiles
    halves = span // LANES
    blocks = place_ref.shape[1]
    pick = (lax.broadcasted_iota(jnp.int32, (cap, blocks), 0) == place_ref[...]).astype(jnp.bfloat16)
    for unit in range(units):
        stacked = jnp.concatenate(
            [left_ref[unit, :, pl.ds(t * span, span)] for t in range(tiles)], axis=0
        )
        packed = jnp.dot(pick, stacked, preferred_element_type=jnp.float32).astype(jnp.bfloat16)
        for half in range(halves):
            out_ref[half, 0, :, pl.ds(unit * LANES, LANES)] = packed[
                :, half * LANES : (half + 1) * LANES
            ]


def mix_kernel(steps, weights_ref, sent_ref, out_ref):
    height = out_ref.shape[0] // steps

    @pl.loop(0, steps)
    def _(i):
        rows = pl.ds(pl.multiple_of(i * height, height), height)
        out_ref[rows, :] = jnp.dot(
            weights_ref[rows, :], sent_ref[...], preferred_element_type=jnp.float32
        ).astype(jnp.bfloat16)


def finish_kernel(tiles, place_ref, alive_ref, back_ref, local_ref, *rest):
    out_ref = rest[-1]
    cap = back_ref.shape[2]
    units, slabs, rows = out_ref.shape
    span = rows // tiles
    halves = span // LANES
    blocks = place_ref.shape[0]
    put = (place_ref[...] == lax.broadcasted_iota(jnp.int32, (blocks, cap), 1)).astype(jnp.bfloat16)
    for unit in range(units):
        packed = jnp.concatenate(
            [back_ref[half, 0, :, pl.ds(unit * LANES, LANES)] for half in range(halves)], axis=1
        )
        spread = jnp.dot(put, packed, preferred_element_type=jnp.float32)
        for t in range(tiles):
            here = pl.ds(t * span, span)
            total = local_ref[unit, :, here] + spread[t * slabs : (t + 1) * slabs]
            out_ref[unit, :, here] = jnp.where(alive_ref[:, here] > 0, total, 0.0).astype(
                jnp.bfloat16
            )


def local_kernel(
    first_tile, live_ref, left_ref, right_ref, vv_ref, pair_ref, occ_ref, before_ref, *rest
):
    local_ref, dens_ref, lf, rf, of = rest[-5:]
    feature, slabs, span = left_ref.shape
    halves = span // LANES
    tile, group = pl.program_id(0), pl.program_id(1)

    @pl.when((tile == 0) & (group == 0))
    def _():
        dens_ref[...] = before_ref[...]

    step = 10 if feature % 10 == 0 else 1

    @pl.loop(0, feature // step)
    def _(i):
        there = pl.ds(pl.multiple_of(i * step * slabs, slabs), step * slabs)
        here = pl.ds(i * step, step)
        for h in range(halves):
            lanes = pl.ds(h * LANES, LANES)
            lf[h, there, :] = left_ref[here, :, lanes].astype(jnp.float32).reshape(-1, LANES)
            rf[h, there, :] = right_ref[here, :, lanes].astype(jnp.float32).reshape(-1, LANES)

    @pl.loop(0, slabs)
    def _(b):
        @pl.when(live_ref[first_tile + tile, group * slabs + b] > 0)
        def _():
            mine = pl.ds(b, feature, stride=slabs)
            lb = jnp.concatenate([lf[h, mine, :] for h in range(halves)], axis=1).astype(jnp.bfloat16)
            rb = jnp.concatenate([rf[h, mine, :] for h in range(halves)], axis=1).astype(jnp.bfloat16)
            dens_ref[...] += lax.dot_general(
                lb, rb, (((1,), (1,)), ((), ())), preferred_element_type=jnp.float32
            )
            term = jnp.dot(vv_ref[...], lb, preferred_element_type=jnp.float32)
            term += occ_ref[...] * pair_ref[pl.ds(b, 1), :]
            for h in range(halves):
                of[h, mine, :] = term[:, h * LANES : (h + 1) * LANES]

    @pl.loop(0, feature // step)
    def _(i):
        there = pl.ds(pl.multiple_of(i * step * slabs, slabs), step * slabs)
        for h in range(halves):
            local_ref[pl.ds(i * step, step), :, pl.ds(h * LANES, LANES)] = of[h, there, :].reshape(
                step, slabs, LANES
            )


def chunking(feature, parts):
    need = -(-feature // parts)
    sub = next(size for size in (5, 4, 3, 2, 1) if feature % size == 0)
    total = -(-need // sub)
    ends = max(1, total // 15)
    inner = [(total - 2 * ends + k) // 4 for k in range(4)]
    cuts = [c for c in [ends, inner[0], inner[1], inner[3], inner[2], ends] if c]
    starts = [sum(cuts[:i]) for i in range(len(cuts))]
    return sub, total, list(zip(starts, cuts))


def after(x, *others):
    return lax.optimization_barrier((x,) + others)[0]


def local_terms(tile_range, live, left, right, vv_turned, picked, occ_rows, dens, local):
    feature, slabs, rows = left.shape
    first_tile, tiles = tile_range
    span = rows // live.shape[0]
    group = 16
    operands = [live, left, right, vv_turned, picked, occ_rows, dens]
    block = pl.BlockSpec((feature, group, span), lambda t, g, live: (0, g, t + first_tile))
    whole = pl.BlockSpec((feature, feature), lambda t, g, live: (0, 0))
    specs = [
        block,
        block,
        whole,
        pl.BlockSpec((group, span), lambda t, g, live: (g, t + first_tile)),
        pl.BlockSpec((feature, span), lambda t, g, live: (0, t + first_tile)),
        whole,
    ]
    aliases = {}
    if local is not None:
        operands.append(local)
        specs.append(pl.BlockSpec(memory_space=pl.ANY))
        aliases = {7: 0}
    halves = span // LANES
    return pl.pallas_call(
        functools.partial(local_kernel, first_tile),
        grid_spec=pltpu.PrefetchScalarGridSpec(
            num_scalar_prefetch=1,
            grid=(tiles, slabs // group),
            in_specs=specs,
            out_specs=[block, whole],
            scratch_shapes=[pltpu.VMEM((halves, feature * group, LANES), jnp.float32)] * 3,
        ),
        out_shape=[
            jax.ShapeDtypeStruct((feature, slabs, rows), jnp.float32),
            jax.ShapeDtypeStruct((feature, feature), jnp.float32),
        ],
        input_output_aliases=aliases,
        compiler_params=pltpu.CompilerParams(vmem_limit_bytes=VMEM_BYTES),
        cost_estimate=pl.CostEstimate(
            flops=4 * feature * feature * slabs * span * tiles,
            bytes_accessed=8 * feature * slabs * span * tiles,
            transcendentals=0,
        ),
        name="local_terms",
    )(*operands)


def packed_plan(cap, sizes, left, right, live, place, tables, vv_block, slab_block, left_doubles,
                ov_block, pair_index, occ_index):
    feature, slabs, rows, tiles, count = sizes
    span = rows // tiles
    halves = span // LANES
    parts = count // halves
    sub, total, chunks = chunking(feature, parts)
    last = feature // sub - 1
    blocks = tiles * slabs
    params = pltpu.CompilerParams(vmem_limit_bytes=VMEM_BYTES)

    def spot(first):
        return lambda q, j: (jnp.minimum(q * total + first + j, last), 0, 0)

    def exchange(x):
        return lax.all_to_all(x, "tile", split_axis=0, concat_axis=0, tiled=True)

    def pack(chunk, place):
        first, width = chunk
        return pl.pallas_call(
            functools.partial(pack_kernel, tiles),
            grid=(parts, width),
            in_specs=[
                pl.BlockSpec((1, blocks), lambda q, j: (0, 0)),
                pl.BlockSpec((sub, slabs, rows), spot(first)),
            ],
            out_specs=pl.BlockSpec((halves, 1, cap, sub * LANES), lambda q, j: (0, q, 0, j)),
            out_shape=jax.ShapeDtypeStruct((halves, parts, cap, width * sub * LANES), jnp.bfloat16),
            compiler_params=params,
            cost_estimate=pl.CostEstimate(
                flops=2 * parts * width * sub * cap * blocks * span,
                bytes_accessed=2 * parts * width * sub * (slabs * rows + cap * span),
                transcendentals=0,
            ),
            name="pack",
        )(place[None, :], left).reshape(count, cap, width * sub * LANES)

    def mix(chunk, weights, sent):
        width = chunk[1]
        height = count * cap
        return pl.pallas_call(
            functools.partial(mix_kernel, count // 2),
            grid=(width,),
            in_specs=[
                pl.BlockSpec((height, height), lambda j: (0, 0)),
                pl.BlockSpec((height, sub * LANES), lambda j: (0, j)),
            ],
            out_specs=pl.BlockSpec((height, sub * LANES), lambda j: (0, j)),
            out_shape=jax.ShapeDtypeStruct((height, width * sub * LANES), jnp.bfloat16),
            compiler_params=params,
            cost_estimate=pl.CostEstimate(
                flops=2 * height * height * width * sub * LANES,
                bytes_accessed=2 * height * (height + 2 * width * sub * LANES),
                transcendentals=0,
            ),
            name="mix",
        )(weights, sent.reshape(height, -1)).reshape(count, cap, -1)

    def finish(chunk, back, local, sigma):
        first, width = chunk
        operands = [place[:, None], alive, back.reshape(halves, parts, cap, -1), local]
        specs = [
            pl.BlockSpec((blocks, 1), lambda q, j: (0, 0)),
            pl.BlockSpec((slabs, rows), lambda q, j: (0, 0)),
            pl.BlockSpec((halves, 1, cap, sub * LANES), lambda q, j: (0, q, 0, j)),
            pl.BlockSpec((sub, slabs, rows), spot(first)),
        ]
        if sigma is not None:
            operands.append(sigma)
            specs.append(pl.BlockSpec(memory_space=pl.ANY))
        return pl.pallas_call(
            functools.partial(finish_kernel, tiles),
            grid=(parts, width),
            in_specs=specs,
            out_specs=pl.BlockSpec((sub, slabs, rows), spot(first)),
            out_shape=jax.ShapeDtypeStruct((feature, slabs, rows), jnp.bfloat16),
            input_output_aliases={} if sigma is None else {4: 0},
            compiler_params=params,
            cost_estimate=pl.CostEstimate(
                flops=2 * parts * width * sub * cap * blocks * span,
                bytes_accessed=parts * width * sub * (6 * slabs * rows + 2 * cap * span),
                transcendentals=0,
            ),
            name="finish",
        )(*operands)

    full_table = lax.all_gather(left_doubles, "grp", axis=1, tiled=True)
    picked = jnp.take(full_table, pair_index, axis=1).astype(jnp.float32)
    occ_hot = (
        jnp.arange(ov_block.shape[0], dtype=jnp.int32)[:, None] == occ_index[None, :]
    ).astype(jnp.bfloat16)
    occ_rows = lax.dot_general(
        ov_block, occ_hot, (((0,), (0,)), ((), ())), preferred_element_type=jnp.float32
    )
    vv_turned = vv_block.T
    pieces = 3 if tiles % 3 == 0 else 1
    piece = tiles // pieces

    count_chunks = len(chunks)
    dens = jnp.zeros((feature, feature), jnp.float32)
    local = None
    begun = 0
    sent = []
    packed = pack(chunks[0], place)
    for i in range(count_chunks):
        gates = [sent[-1]] if sent else []
        sent.append(exchange(after(packed, *gates)))
        if i + 1 < count_chunks:
            if local is not None:
                gates = gates + [dens]
            packed = pack(chunks[i + 1], after(place, *gates))
        if i >= 1 and begun < pieces:
            local, dens = local_terms(
                (begun * piece, piece), after(live.T, packed), left, right, vv_turned, picked,
                occ_rows, dens, local,
            )
            begun += 1
    while begun < pieces:
        local, dens = local_terms(
            (begun * piece, piece), live.T, left, right, vv_turned, picked, occ_rows, dens, local
        )
        begun += 1
    norm_scale = math.sqrt(slabs * count * rows * lax.axis_size("grp"))
    swaps = [
        (axis, 1 << bit)
        for axis in ("grp", "tile")
        for bit in range((lax.axis_size(axis) - 1).bit_length())
    ]

    def add_swapped(x, swap, *gates):
        axis, bit = swap
        pairs = [(k, k ^ bit) for k in range(lax.axis_size(axis))]
        return x + lax.ppermute(after(x, *gates), axis, pairs)

    entry = jnp.arange(blocks, dtype=jnp.int32)
    hit = tables[:, None, :] == jnp.arange(cap, dtype=jnp.int32)[None, :, None]
    index = jnp.sum(jnp.where(hit, entry[None, None, :] + 1, 0), axis=2) - 1
    owner = jnp.arange(count, dtype=jnp.int32)[:, None]
    slab_of = jnp.where(index >= 0, index % slabs + owner * slabs, -1).reshape(-1)
    tile_of = (index // slabs).reshape(-1)
    onehot = (
        slab_of[:, None] == jnp.arange(slab_block.shape[0], dtype=jnp.int32)[None, :]
    ).astype(jnp.bfloat16)
    picked_rows = jnp.dot(onehot, slab_block, preferred_element_type=jnp.float32).astype(jnp.bfloat16)
    weights = lax.dot_general(
        picked_rows, onehot, (((1,), (1,)), ((), ())), preferred_element_type=jnp.float32
    )
    weights = jnp.where(tile_of[:, None] == tile_of[None, :], weights, 0.0).astype(jnp.bfloat16)

    alive = jnp.repeat(live.astype(jnp.float32), span, axis=1)
    sigma = None
    backs = []
    for i in range(count_chunks):
        mixed = mix(chunks[i], weights, sent[i])
        gates = [backs[-1]] if i >= 1 else [sent[-1]]
        if i >= 1:
            gates.append(dens)
        if i >= 2:
            sigma = finish(chunks[i - 2], backs[i - 2], local, sigma)
            mixed, sigma = lax.optimization_barrier((mixed, sigma) + tuple(gates))[:2]
        else:
            mixed = after(mixed, *gates)
        backs.append(exchange(mixed))
        if swaps:
            dens = add_swapped(dens, swaps.pop(0), *gates[:1])
    for swap in swaps:
        dens = add_swapped(dens, swap)
    density = dens / norm_scale
    for i in range(max(0, count_chunks - 2), count_chunks):
        back = backs[i]
        if i == count_chunks - 1:
            back, density = lax.optimization_barrier((back, density))
        sigma = finish(chunks[i], back, local, sigma)
    return sigma, density


def caps_of(blocks):
    marks = [80, 88, 96, 104, 112]
    return [m for m in marks if m < blocks] + [-(-blocks // 16) * 16]


def body(
    left_triples,
    right_triples,
    live_tiles,
    vv_block,
    slab_block,
    left_doubles,
    ov_block,
    pair_index,
    occ_index,
):
    slabs, rows, feature = left_triples.shape
    tiles = live_tiles.shape[1]
    count = lax.axis_size("tile")
    sizes = (feature, slabs, rows, tiles, count)
    left = jnp.transpose(left_triples, (2, 0, 1))
    right = jnp.transpose(right_triples, (2, 0, 1))

    own = live_tiles.T.reshape(-1)
    place = jnp.where(own > 0, jnp.cumsum(own) - 1, -1)
    devices = count * lax.axis_size("grp")
    everyone = lax.all_to_all(
        jnp.broadcast_to(place, (devices, 1, tiles * slabs)), ("tile", "grp"), 0, 0, tiled=True
    )
    most = jnp.max(everyone) + 1
    tables = lax.dynamic_index_in_dim(
        everyone.reshape(count, -1, tiles * slabs), lax.axis_index("grp"), 1, keepdims=False
    )

    caps = caps_of(tiles * slabs)
    which = jnp.sum((most > jnp.array(caps[:-1], jnp.int32)).astype(jnp.int32))
    sigma, density = lax.switch(
        which,
        [functools.partial(packed_plan, cap, sizes) for cap in caps],
        left, right, live_tiles, place, tables, vv_block, slab_block, left_doubles,
        ov_block, pair_index, occ_index,
    )
    return jnp.transpose(sigma, (1, 2, 0)), density


def takes_packed(mesh, shape, tiles):
    slabs, rows = shape[0] // mesh.shape["tile"], shape[1] // mesh.shape["grp"]
    local_tiles = tiles // mesh.shape["grp"]
    span = rows // local_tiles
    return slabs % 16 == 0 and span % LANES == 0 and mesh.shape["tile"] % (span // LANES) == 0


def solution(mesh):
    in_specs = (
        P("tile", "grp", None),
        P("tile", "grp", None),
        P("tile", "grp"),
        P(),
        P(),
        P("tile", "grp"),
        P(),
        P("grp"),
        P("grp"),
    )
    out_specs = (P("tile", "grp", None), P())

    def program(left_triples, right_triples, live_tiles, *others):
        packed = takes_packed(mesh, left_triples.shape, live_tiles.shape[1])
        mapped = jax.shard_map(
            body if packed else plain_body,
            mesh=mesh,
            in_specs=in_specs,
            out_specs=out_specs,
            check_vma=False,
        )
        return mapped(left_triples, right_triples, live_tiles, *others)

    return program
```

```python
import functools
import math

import jax
import jax.numpy as jnp
from jax import lax
from jax.experimental import pallas as pl
from jax.experimental.pallas import tpu as pltpu
from jax.sharding import PartitionSpec as P

LANES = 128
VMEM_BYTES = 56 << 20


def plain_body(
    left_triples,
    right_triples,
    live_tiles,
    vv_block,
    slab_block,
    left_doubles,
    ov_block,
    pair_index,
    occ_index,
):
    slab_count, row_count, feature = left_triples.shape
    tile_count = live_tiles.shape[1]
    tile_rows = row_count // tile_count
    live_mask = live_tiles.astype(jnp.bfloat16)
    masked = (
        left_triples.reshape(slab_count, tile_count, tile_rows, feature)
        * live_mask[:, :, None, None]
    ).reshape(slab_count, row_count, feature)
    mixed_rows = jnp.einsum(
        "bd,drc->brc",
        slab_block,
        lax.all_to_all(masked, "tile", split_axis=1, concat_axis=0, tiled=True),
        preferred_element_type=jnp.float32,
    ).astype(jnp.bfloat16)
    slab_term = lax.all_to_all(mixed_rows, "tile", split_axis=0, concat_axis=1, tiled=True)
    full_table = lax.all_gather(left_doubles, "grp", axis=1, tiled=True)
    picked = jnp.take(full_table, pair_index, axis=1).astype(jnp.float32)
    onehot = (occ_index[:, None] == jnp.arange(ov_block.shape[0], dtype=jnp.int32)[None, :]).astype(
        jnp.bfloat16
    )
    occ_rows = jnp.dot(onehot, ov_block, preferred_element_type=jnp.float32)
    pair_term = picked[:, :, None] * occ_rows[None, :, :]
    flat_rows = masked.reshape(-1, feature)
    vv_term = jnp.dot(flat_rows, vv_block, preferred_element_type=jnp.float32).reshape(
        slab_count, row_count, feature
    )
    partial_value = lax.dot_general(
        flat_rows,
        right_triples.reshape(-1, feature),
        (((0,), (0,)), ((), ())),
        preferred_element_type=jnp.float32,
    )
    summed = vv_term + slab_term.astype(jnp.float32) + pair_term
    summed = (
        summed.reshape(slab_count, tile_count, tile_rows, feature)
        * live_tiles.astype(jnp.float32)[:, :, None, None]
    )
    sigma_out = summed.reshape(slab_count, row_count, feature).astype(jnp.bfloat16)
    norm_scale = math.sqrt(slab_count * lax.axis_size("tile") * row_count * lax.axis_size("grp"))
    density = lax.psum(partial_value, ("tile", "grp")) / norm_scale
    return (sigma_out, density)


def pack_kernel(tiles, place_ref, left_ref, out_ref):
    cap = out_ref.shape[2]
    units = left_ref.shape[0]
    span = left_ref.shape[2] // tiles
    halves = span // LANES
    blocks = place_ref.shape[1]
    pick = (lax.broadcasted_iota(jnp.int32, (cap, blocks), 0) == place_ref[...]).astype(jnp.bfloat16)
    for unit in range(units):
        stacked = jnp.concatenate(
            [left_ref[unit, :, pl.ds(t * span, span)] for t in range(tiles)], axis=0
        )
        packed = jnp.dot(pick, stacked, preferred_element_type=jnp.float32).astype(jnp.bfloat16)
        for half in range(halves):
            out_ref[half, 0, :, pl.ds(unit * LANES, LANES)] = packed[
                :, half * LANES : (half + 1) * LANES
            ]


def mix_kernel(steps, weights_ref, sent_ref, out_ref):
    height = out_ref.shape[0] // steps

    @pl.loop(0, steps)
    def _(i):
        rows = pl.ds(pl.multiple_of(i * height, height), height)
        out_ref[rows, :] = jnp.dot(
            weights_ref[rows, :], sent_ref[...], preferred_element_type=jnp.float32
        ).astype(jnp.bfloat16)


def finish_kernel(tiles, place_ref, alive_ref, back_ref, local_ref, *rest):
    out_ref = rest[-1]
    cap = back_ref.shape[2]
    units, slabs, rows = out_ref.shape
    span = rows // tiles
    halves = span // LANES
    blocks = place_ref.shape[0]
    put = (place_ref[...] == lax.broadcasted_iota(jnp.int32, (blocks, cap), 1)).astype(jnp.bfloat16)
    for unit in range(units):
        packed = jnp.concatenate(
            [back_ref[half, 0, :, pl.ds(unit * LANES, LANES)] for half in range(halves)], axis=1
        )
        spread = jnp.dot(put, packed, preferred_element_type=jnp.float32)
        for t in range(tiles):
            here = pl.ds(t * span, span)
            total = local_ref[unit, :, here] + spread[t * slabs : (t + 1) * slabs]
            out_ref[unit, :, here] = jnp.where(alive_ref[:, here] > 0, total, 0.0).astype(
                jnp.bfloat16
            )


def local_kernel(
    first_tile, live_ref, left_ref, right_ref, vv_ref, pair_ref, occ_ref, before_ref, *rest
):
    local_ref, dens_ref, lf, rf, of = rest[-5:]
    feature, slabs, span = left_ref.shape
    halves = span // LANES
    tile, group = pl.program_id(0), pl.program_id(1)

    @pl.when((tile == 0) & (group == 0))
    def _():
        dens_ref[...] = before_ref[...]

    step = 10 if feature % 10 == 0 else 1

    @pl.loop(0, feature // step)
    def _(i):
        there = pl.ds(pl.multiple_of(i * step * slabs, slabs), step * slabs)
        here = pl.ds(i * step, step)
        for h in range(halves):
            lanes = pl.ds(h * LANES, LANES)
            lf[h, there, :] = left_ref[here, :, lanes].astype(jnp.float32).reshape(-1, LANES)
            rf[h, there, :] = right_ref[here, :, lanes].astype(jnp.float32).reshape(-1, LANES)

    @pl.loop(0, slabs)
    def _(b):
        @pl.when(live_ref[first_tile + tile, group * slabs + b] > 0)
        def _():
            mine = pl.ds(b, feature, stride=slabs)
            lb = jnp.concatenate([lf[h, mine, :] for h in range(halves)], axis=1).astype(jnp.bfloat16)
            rb = jnp.concatenate([rf[h, mine, :] for h in range(halves)], axis=1).astype(jnp.bfloat16)
            dens_ref[...] += lax.dot_general(
                lb, rb, (((1,), (1,)), ((), ())), preferred_element_type=jnp.float32
            )
            term = jnp.dot(vv_ref[...], lb, preferred_element_type=jnp.float32)
            term += occ_ref[...] * pair_ref[pl.ds(b, 1), :]
            for h in range(halves):
                of[h, mine, :] = term[:, h * LANES : (h + 1) * LANES]

    @pl.loop(0, feature // step)
    def _(i):
        there = pl.ds(pl.multiple_of(i * step * slabs, slabs), step * slabs)
        for h in range(halves):
            local_ref[pl.ds(i * step, step), :, pl.ds(h * LANES, LANES)] = of[h, there, :].reshape(
                step, slabs, LANES
            )


def chunking(feature, parts):
    need = -(-feature // parts)
    sub = next(size for size in (5, 4, 3, 2, 1) if feature % size == 0)
    total = -(-need // sub)
    ends = min(2, -(-total // 7))
    cuts = [c for c in (ends, total - 2 * ends, ends) if c > 0]
    starts = [sum(cuts[:i]) for i in range(len(cuts))]
    return sub, total, list(zip(starts, cuts))


def after(x, *others):
    return lax.optimization_barrier((x,) + others)[0]


def local_terms(tile_range, live, left, right, vv_turned, picked, occ_rows, dens, local):
    feature, slabs, rows = left.shape
    first_tile, tiles = tile_range
    span = rows // live.shape[0]
    group = 16
    operands = [live, left, right, vv_turned, picked, occ_rows, dens]
    block = pl.BlockSpec((feature, group, span), lambda t, g, live: (0, g, t + first_tile))
    whole = pl.BlockSpec((feature, feature), lambda t, g, live: (0, 0))
    specs = [
        block,
        block,
        whole,
        pl.BlockSpec((group, span), lambda t, g, live: (g, t + first_tile)),
        pl.BlockSpec((feature, span), lambda t, g, live: (0, t + first_tile)),
        whole,
    ]
    aliases = {}
    if local is not None:
        operands.append(local)
        specs.append(pl.BlockSpec(memory_space=pl.ANY))
        aliases = {7: 0}
    halves = span // LANES
    return pl.pallas_call(
        functools.partial(local_kernel, first_tile),
        grid_spec=pltpu.PrefetchScalarGridSpec(
            num_scalar_prefetch=1,
            grid=(tiles, slabs // group),
            in_specs=specs,
            out_specs=[block, whole],
            scratch_shapes=[pltpu.VMEM((halves, feature * group, LANES), jnp.float32)] * 3,
        ),
        out_shape=[
            jax.ShapeDtypeStruct((feature, slabs, rows), jnp.float32),
            jax.ShapeDtypeStruct((feature, feature), jnp.float32),
        ],
        input_output_aliases=aliases,
        compiler_params=pltpu.CompilerParams(vmem_limit_bytes=VMEM_BYTES),
        cost_estimate=pl.CostEstimate(
            flops=4 * feature * feature * slabs * span * tiles,
            bytes_accessed=8 * feature * slabs * span * tiles,
            transcendentals=0,
        ),
        name="local_terms",
    )(*operands)


def packed_plan(cap, sizes, left, right, live, place, tables, vv_block, slab_block, left_doubles,
                ov_block, pair_index, occ_index):
    feature, slabs, rows, tiles, count = sizes
    span = rows // tiles
    halves = span // LANES
    parts = count // halves
    sub, total, chunks = chunking(feature, parts)
    last = feature // sub - 1
    blocks = tiles * slabs
    params = pltpu.CompilerParams(vmem_limit_bytes=VMEM_BYTES)

    def spot(first):
        return lambda q, j: (jnp.minimum(q * total + first + j, last), 0, 0)

    def exchange(x):
        return lax.all_to_all(x, "tile", split_axis=0, concat_axis=0, tiled=True)

    def pack(chunk, place):
        first, width = chunk
        return pl.pallas_call(
            functools.partial(pack_kernel, tiles),
            grid=(parts, width),
            in_specs=[
                pl.BlockSpec((1, blocks), lambda q, j: (0, 0)),
                pl.BlockSpec((sub, slabs, rows), spot(first)),
            ],
            out_specs=pl.BlockSpec((halves, 1, cap, sub * LANES), lambda q, j: (0, q, 0, j)),
            out_shape=jax.ShapeDtypeStruct((halves, parts, cap, width * sub * LANES), jnp.bfloat16),
            compiler_params=params,
            cost_estimate=pl.CostEstimate(
                flops=2 * parts * width * sub * cap * blocks * span,
                bytes_accessed=2 * parts * width * sub * (slabs * rows + cap * span),
                transcendentals=0,
            ),
            name="pack",
        )(place[None, :], left).reshape(count, cap, width * sub * LANES)

    def mix(chunk, weights, sent):
        width = chunk[1]
        height = count * cap
        return pl.pallas_call(
            functools.partial(mix_kernel, count // 2),
            grid=(width,),
            in_specs=[
                pl.BlockSpec((height, height), lambda j: (0, 0)),
                pl.BlockSpec((height, sub * LANES), lambda j: (0, j)),
            ],
            out_specs=pl.BlockSpec((height, sub * LANES), lambda j: (0, j)),
            out_shape=jax.ShapeDtypeStruct((height, width * sub * LANES), jnp.bfloat16),
            compiler_params=params,
            cost_estimate=pl.CostEstimate(
                flops=2 * height * height * width * sub * LANES,
                bytes_accessed=2 * height * (height + 2 * width * sub * LANES),
                transcendentals=0,
            ),
            name="mix",
        )(weights, sent.reshape(height, -1)).reshape(count, cap, -1)

    def finish(chunk, back, local, sigma):
        first, width = chunk
        operands = [place[:, None], alive, back.reshape(halves, parts, cap, -1), local]
        specs = [
            pl.BlockSpec((blocks, 1), lambda q, j: (0, 0)),
            pl.BlockSpec((slabs, rows), lambda q, j: (0, 0)),
            pl.BlockSpec((halves, 1, cap, sub * LANES), lambda q, j: (0, q, 0, j)),
            pl.BlockSpec((sub, slabs, rows), spot(first)),
        ]
        if sigma is not None:
            operands.append(sigma)
            specs.append(pl.BlockSpec(memory_space=pl.ANY))
        return pl.pallas_call(
            functools.partial(finish_kernel, tiles),
            grid=(parts, width),
            in_specs=specs,
            out_specs=pl.BlockSpec((sub, slabs, rows), spot(first)),
            out_shape=jax.ShapeDtypeStruct((feature, slabs, rows), jnp.bfloat16),
            input_output_aliases={} if sigma is None else {4: 0},
            compiler_params=params,
            cost_estimate=pl.CostEstimate(
                flops=2 * parts * width * sub * cap * blocks * span,
                bytes_accessed=parts * width * sub * (6 * slabs * rows + 2 * cap * span),
                transcendentals=0,
            ),
            name="finish",
        )(*operands)

    full_table = lax.all_gather(left_doubles, "grp", axis=1, tiled=True)
    picked = jnp.take(full_table, pair_index, axis=1).astype(jnp.float32)
    occ_hot = (
        jnp.arange(ov_block.shape[0], dtype=jnp.int32)[:, None] == occ_index[None, :]
    ).astype(jnp.bfloat16)
    occ_rows = lax.dot_general(
        ov_block, occ_hot, (((0,), (0,)), ((), ())), preferred_element_type=jnp.float32
    )
    vv_turned = vv_block.T
    pieces = 1
    piece = tiles // pieces

    swaps = [
        (axis, 1 << bit)
        for axis in ("grp", "tile")
        for bit in range((lax.axis_size(axis) - 1).bit_length())
    ]
    early = len(swaps) // 2 + 1

    def add_swapped(x, steps):
        for axis, bit in steps:
            x = x + lax.ppermute(x, axis, [(k, k ^ bit) for k in range(lax.axis_size(axis))])
        return x

    count_chunks = len(chunks)
    dens = jnp.zeros((feature, feature), jnp.float32)
    local = None
    begun = 0
    sent = []
    packed = pack(chunks[0], place)
    for i in range(count_chunks):
        gates = [sent[-1]] if sent else []
        if local is not None:
            gates = gates + [dens]
        sent.append(exchange(after(packed, *gates)))
        if i + 1 < count_chunks:
            packed = pack(chunks[i + 1], after(place, *gates))
        if i >= 1 and begun < pieces:
            local, dens = local_terms(
                (begun * piece, piece), after(live.T, packed), left, right, vv_turned, picked,
                occ_rows, dens, local,
            )
            begun += 1
            if begun == pieces:
                dens = add_swapped(dens, swaps[:early])
    while begun < pieces:
        local, dens = local_terms(
            (begun * piece, piece), live.T, left, right, vv_turned, picked, occ_rows, dens, local
        )
        begun += 1
    if count_chunks < 2:
        dens = add_swapped(dens, swaps[:early])
    norm_scale = math.sqrt(slabs * count * rows * lax.axis_size("grp"))
    dens = add_swapped(after(dens, *sent[:-1]), swaps[early:-1])

    entry = jnp.arange(blocks, dtype=jnp.int32)
    hit = tables[:, None, :] == jnp.arange(cap, dtype=jnp.int32)[None, :, None]
    index = jnp.sum(jnp.where(hit, entry[None, None, :] + 1, 0), axis=2) - 1
    owner = jnp.arange(count, dtype=jnp.int32)[:, None]
    slab_of = jnp.where(index >= 0, index % slabs + owner * slabs, -1).reshape(-1)
    tile_of = (index // slabs).reshape(-1)
    onehot = (
        slab_of[:, None] == jnp.arange(slab_block.shape[0], dtype=jnp.int32)[None, :]
    ).astype(jnp.bfloat16)
    picked_rows = jnp.dot(onehot, slab_block, preferred_element_type=jnp.float32).astype(jnp.bfloat16)
    weights = lax.dot_general(
        picked_rows, onehot, (((1,), (1,)), ((), ())), preferred_element_type=jnp.float32
    )
    weights = jnp.where(tile_of[:, None] == tile_of[None, :], weights, 0.0).astype(jnp.bfloat16)

    alive = jnp.repeat(live.astype(jnp.float32), span, axis=1)
    sigma = None
    backs = []
    for i in range(count_chunks):
        mixed = mix(chunks[i], weights, sent[i])
        gates = [backs[-1]] if i >= 1 else [sent[-1]]
        if i == 0:
            gates.append(dens)
            density = add_swapped(after(dens, sent[-1]), swaps[early:][-1:]) / norm_scale
        elif i == 1:
            gates.append(density)
        if i >= 2:
            sigma = finish(chunks[i - 2], backs[i - 2], local, sigma)
            mixed, sigma = lax.optimization_barrier((mixed, sigma) + tuple(gates))[:2]
        else:
            mixed = after(mixed, *gates)
        backs.append(exchange(mixed))
    for i in range(max(0, count_chunks - 2), count_chunks):
        back = backs[i]
        if i == count_chunks - 1:
            back, density = lax.optimization_barrier((back, density))
        sigma = finish(chunks[i], back, local, sigma)
    return sigma, density


def caps_of(blocks):
    marks = [72, 80, 88, 96, 104, 112, 128]
    return [m for m in marks if m < blocks] + [-(-blocks // 16) * 16]


def body(
    left_triples,
    right_triples,
    live_tiles,
    vv_block,
    slab_block,
    left_doubles,
    ov_block,
    pair_index,
    occ_index,
):
    slabs, rows, feature = left_triples.shape
    tiles = live_tiles.shape[1]
    count = lax.axis_size("tile")
    sizes = (feature, slabs, rows, tiles, count)
    left = jnp.transpose(left_triples, (2, 0, 1))
    right = jnp.transpose(right_triples, (2, 0, 1))

    own = live_tiles.T.reshape(-1)
    place = jnp.where(own > 0, jnp.cumsum(own) - 1, -1)
    devices = count * lax.axis_size("grp")
    everyone = lax.all_to_all(
        jnp.broadcast_to(place, (devices, 1, tiles * slabs)), ("tile", "grp"), 0, 0, tiled=True
    )
    most = jnp.max(everyone) + 1
    tables = lax.dynamic_index_in_dim(
        everyone.reshape(count, -1, tiles * slabs), lax.axis_index("grp"), 1, keepdims=False
    )

    caps = caps_of(tiles * slabs)
    which = jnp.sum((most > jnp.array(caps[:-1], jnp.int32)).astype(jnp.int32))
    sigma, density = lax.switch(
        which,
        [functools.partial(packed_plan, cap, sizes) for cap in caps],
        left, right, live_tiles, place, tables, vv_block, slab_block, left_doubles,
        ov_block, pair_index, occ_index,
    )
    return jnp.transpose(sigma, (1, 2, 0)), density


def takes_packed(mesh, shape, tiles):
    slabs, rows = shape[0] // mesh.shape["tile"], shape[1] // mesh.shape["grp"]
    local_tiles = tiles // mesh.shape["grp"]
    span = rows // local_tiles
    return slabs % 16 == 0 and span % LANES == 0 and mesh.shape["tile"] % (span // LANES) == 0


def solution(mesh):
    in_specs = (
        P("tile", "grp", None),
        P("tile", "grp", None),
        P("tile", "grp"),
        P(),
        P(),
        P("tile", "grp"),
        P(),
        P("grp"),
        P("grp"),
    )
    out_specs = (P("tile", "grp", None), P())

    def program(left_triples, right_triples, live_tiles, *others):
        packed = takes_packed(mesh, left_triples.shape, live_tiles.shape[1])
        mapped = jax.shard_map(
            body if packed else plain_body,
            mesh=mesh,
            in_specs=in_specs,
            out_specs=out_specs,
            check_vma=False,
        )
        return mapped(left_triples, right_triples, live_tiles, *others)

    return program
```

```python
import functools
import math

import jax
import jax.numpy as jnp
from jax import lax
from jax.experimental import pallas as pl
from jax.experimental.pallas import tpu as pltpu
from jax.sharding import PartitionSpec as P

LANES = 128
VMEM_BYTES = 56 << 20


def plain_body(
    left_triples,
    right_triples,
    live_tiles,
    vv_block,
    slab_block,
    left_doubles,
    ov_block,
    pair_index,
    occ_index,
):
    slab_count, row_count, feature = left_triples.shape
    tile_count = live_tiles.shape[1]
    tile_rows = row_count // tile_count
    live_mask = live_tiles.astype(jnp.bfloat16)
    masked = (
        left_triples.reshape(slab_count, tile_count, tile_rows, feature)
        * live_mask[:, :, None, None]
    ).reshape(slab_count, row_count, feature)
    mixed_rows = jnp.einsum(
        "bd,drc->brc",
        slab_block,
        lax.all_to_all(masked, "tile", split_axis=1, concat_axis=0, tiled=True),
        preferred_element_type=jnp.float32,
    ).astype(jnp.bfloat16)
    slab_term = lax.all_to_all(mixed_rows, "tile", split_axis=0, concat_axis=1, tiled=True)
    full_table = lax.all_gather(left_doubles, "grp", axis=1, tiled=True)
    picked = jnp.take(full_table, pair_index, axis=1).astype(jnp.float32)
    onehot = (occ_index[:, None] == jnp.arange(ov_block.shape[0], dtype=jnp.int32)[None, :]).astype(
        jnp.bfloat16
    )
    occ_rows = jnp.dot(onehot, ov_block, preferred_element_type=jnp.float32)
    pair_term = picked[:, :, None] * occ_rows[None, :, :]
    flat_rows = masked.reshape(-1, feature)
    vv_term = jnp.dot(flat_rows, vv_block, preferred_element_type=jnp.float32).reshape(
        slab_count, row_count, feature
    )
    partial_value = lax.dot_general(
        flat_rows,
        right_triples.reshape(-1, feature),
        (((0,), (0,)), ((), ())),
        preferred_element_type=jnp.float32,
    )
    summed = vv_term + slab_term.astype(jnp.float32) + pair_term
    summed = (
        summed.reshape(slab_count, tile_count, tile_rows, feature)
        * live_tiles.astype(jnp.float32)[:, :, None, None]
    )
    sigma_out = summed.reshape(slab_count, row_count, feature).astype(jnp.bfloat16)
    norm_scale = math.sqrt(slab_count * lax.axis_size("tile") * row_count * lax.axis_size("grp"))
    density = lax.psum(partial_value, ("tile", "grp")) / norm_scale
    return (sigma_out, density)


def pack_kernel(tiles, place_ref, left_ref, out_ref):
    cap = out_ref.shape[2]
    units = left_ref.shape[0]
    span = left_ref.shape[2] // tiles
    halves = span // LANES
    blocks = place_ref.shape[1]
    pick = (lax.broadcasted_iota(jnp.int32, (cap, blocks), 0) == place_ref[...]).astype(jnp.bfloat16)
    for unit in range(units):
        stacked = jnp.concatenate(
            [left_ref[unit, :, pl.ds(t * span, span)] for t in range(tiles)], axis=0
        )
        packed = jnp.dot(pick, stacked, preferred_element_type=jnp.float32).astype(jnp.bfloat16)
        for half in range(halves):
            out_ref[half, 0, :, pl.ds(unit * LANES, LANES)] = packed[
                :, half * LANES : (half + 1) * LANES
            ]


def mix_kernel(steps, weights_ref, sent_ref, out_ref):
    height = out_ref.shape[0] // steps

    @pl.loop(0, steps)
    def _(i):
        rows = pl.ds(pl.multiple_of(i * height, height), height)
        out_ref[rows, :] = jnp.dot(
            weights_ref[rows, :], sent_ref[...], preferred_element_type=jnp.float32
        ).astype(jnp.bfloat16)


def finish_kernel(tiles, place_ref, alive_ref, back_ref, local_ref, *rest):
    out_ref = rest[-1]
    cap = back_ref.shape[2]
    units, slabs, rows = out_ref.shape
    span = rows // tiles
    halves = span // LANES
    blocks = place_ref.shape[0]
    put = (place_ref[...] == lax.broadcasted_iota(jnp.int32, (blocks, cap), 1)).astype(jnp.bfloat16)
    for unit in range(units):
        packed = jnp.concatenate(
            [back_ref[half, 0, :, pl.ds(unit * LANES, LANES)] for half in range(halves)], axis=1
        )
        spread = jnp.dot(put, packed, preferred_element_type=jnp.float32)
        for t in range(tiles):
            here = pl.ds(t * span, span)
            total = local_ref[unit, :, here] + spread[t * slabs : (t + 1) * slabs]
            out_ref[unit, :, here] = jnp.where(alive_ref[:, here] > 0, total, 0.0).astype(
                jnp.bfloat16
            )


def local_kernel(
    first_tile, live_ref, left_ref, right_ref, vv_ref, pair_ref, occ_ref, before_ref, *rest
):
    local_ref, dens_ref, lf, rf, of = rest[-5:]
    feature, slabs, span = left_ref.shape
    halves = span // LANES
    tile, group = pl.program_id(0), pl.program_id(1)

    @pl.when((tile == 0) & (group == 0))
    def _():
        dens_ref[...] = before_ref[...]

    step = 10 if feature % 10 == 0 else 1

    @pl.loop(0, feature // step)
    def _(i):
        there = pl.ds(pl.multiple_of(i * step * slabs, slabs), step * slabs)
        here = pl.ds(i * step, step)
        for h in range(halves):
            lanes = pl.ds(h * LANES, LANES)
            lf[h, there, :] = left_ref[here, :, lanes].astype(jnp.float32).reshape(-1, LANES)
            rf[h, there, :] = right_ref[here, :, lanes].astype(jnp.float32).reshape(-1, LANES)

    @pl.loop(0, slabs)
    def _(b):
        @pl.when(live_ref[first_tile + tile, group * slabs + b] > 0)
        def _():
            mine = pl.ds(b, feature, stride=slabs)
            lb = jnp.concatenate([lf[h, mine, :] for h in range(halves)], axis=1).astype(jnp.bfloat16)
            rb = jnp.concatenate([rf[h, mine, :] for h in range(halves)], axis=1).astype(jnp.bfloat16)
            dens_ref[...] += lax.dot_general(
                lb, rb, (((1,), (1,)), ((), ())), preferred_element_type=jnp.float32
            )
            term = jnp.dot(vv_ref[...], lb, preferred_element_type=jnp.float32)
            term += occ_ref[...] * pair_ref[pl.ds(b, 1), :]
            for h in range(halves):
                of[h, mine, :] = term[:, h * LANES : (h + 1) * LANES]

    @pl.loop(0, feature // step)
    def _(i):
        there = pl.ds(pl.multiple_of(i * step * slabs, slabs), step * slabs)
        for h in range(halves):
            local_ref[pl.ds(i * step, step), :, pl.ds(h * LANES, LANES)] = of[h, there, :].reshape(
                step, slabs, LANES
            )


def chunking(feature, parts):
    need = -(-feature // parts)
    sub = next(size for size in (5, 4, 3, 2, 1) if feature % size == 0)
    total = -(-need // sub)
    ends = min(2, -(-total // 7))
    cuts = [c for c in (ends, total - 2 * ends, ends) if c > 0]
    starts = [sum(cuts[:i]) for i in range(len(cuts))]
    return sub, total, list(zip(starts, cuts))


def after(x, *others):
    return lax.optimization_barrier((x,) + others)[0]


def local_terms(tile_range, live, left, right, vv_turned, picked, occ_rows, dens, local):
    feature, slabs, rows = left.shape
    first_tile, tiles = tile_range
    span = rows // live.shape[0]
    group = 16
    operands = [live, left, right, vv_turned, picked, occ_rows, dens]
    block = pl.BlockSpec((feature, group, span), lambda t, g, live: (0, g, t + first_tile))
    whole = pl.BlockSpec((feature, feature), lambda t, g, live: (0, 0))
    specs = [
        block,
        block,
        whole,
        pl.BlockSpec((group, span), lambda t, g, live: (g, t + first_tile)),
        pl.BlockSpec((feature, span), lambda t, g, live: (0, t + first_tile)),
        whole,
    ]
    aliases = {}
    if local is not None:
        operands.append(local)
        specs.append(pl.BlockSpec(memory_space=pl.ANY))
        aliases = {7: 0}
    halves = span // LANES
    return pl.pallas_call(
        functools.partial(local_kernel, first_tile),
        grid_spec=pltpu.PrefetchScalarGridSpec(
            num_scalar_prefetch=1,
            grid=(tiles, slabs // group),
            in_specs=specs,
            out_specs=[block, whole],
            scratch_shapes=[pltpu.VMEM((halves, feature * group, LANES), jnp.float32)] * 3,
        ),
        out_shape=[
            jax.ShapeDtypeStruct((feature, slabs, rows), jnp.float32),
            jax.ShapeDtypeStruct((feature, feature), jnp.float32),
        ],
        input_output_aliases=aliases,
        compiler_params=pltpu.CompilerParams(vmem_limit_bytes=VMEM_BYTES),
        cost_estimate=pl.CostEstimate(
            flops=4 * feature * feature * slabs * span * tiles,
            bytes_accessed=8 * feature * slabs * span * tiles,
            transcendentals=0,
        ),
        name="local_terms",
    )(*operands)


def packed_plan(cap, sizes, left, right, live, place, tables, vv_block, slab_block, left_doubles,
                ov_block, pair_index, occ_index):
    feature, slabs, rows, tiles, count = sizes
    span = rows // tiles
    halves = span // LANES
    parts = count // halves
    sub, total, chunks = chunking(feature, parts)
    last = feature // sub - 1
    blocks = tiles * slabs
    params = pltpu.CompilerParams(vmem_limit_bytes=VMEM_BYTES)

    def spot(first):
        return lambda q, j: (jnp.minimum(q * total + first + j, last), 0, 0)

    def exchange(x):
        return lax.all_to_all(x, "tile", split_axis=0, concat_axis=0, tiled=True)

    def pack(chunk, place):
        first, width = chunk
        return pl.pallas_call(
            functools.partial(pack_kernel, tiles),
            grid=(parts, width),
            in_specs=[
                pl.BlockSpec((1, blocks), lambda q, j: (0, 0)),
                pl.BlockSpec((sub, slabs, rows), spot(first)),
            ],
            out_specs=pl.BlockSpec((halves, 1, cap, sub * LANES), lambda q, j: (0, q, 0, j)),
            out_shape=jax.ShapeDtypeStruct((halves, parts, cap, width * sub * LANES), jnp.bfloat16),
            compiler_params=params,
            cost_estimate=pl.CostEstimate(
                flops=2 * parts * width * sub * cap * blocks * span,
                bytes_accessed=2 * parts * width * sub * (slabs * rows + cap * span),
                transcendentals=0,
            ),
            name="pack",
        )(place[None, :], left).reshape(count, cap, width * sub * LANES)

    def mix(chunk, weights, sent):
        width = chunk[1]
        height = count * cap
        return pl.pallas_call(
            functools.partial(mix_kernel, count // 2),
            grid=(width,),
            in_specs=[
                pl.BlockSpec((height, height), lambda j: (0, 0)),
                pl.BlockSpec((height, sub * LANES), lambda j: (0, j)),
            ],
            out_specs=pl.BlockSpec((height, sub * LANES), lambda j: (0, j)),
            out_shape=jax.ShapeDtypeStruct((height, width * sub * LANES), jnp.bfloat16),
            compiler_params=params,
            cost_estimate=pl.CostEstimate(
                flops=2 * height * height * width * sub * LANES,
                bytes_accessed=2 * height * (height + 2 * width * sub * LANES),
                transcendentals=0,
            ),
            name="mix",
        )(weights, sent.reshape(height, -1)).reshape(count, cap, -1)

    def finish(chunk, back, local, sigma):
        first, width = chunk
        operands = [place[:, None], alive, back.reshape(halves, parts, cap, -1), local]
        specs = [
            pl.BlockSpec((blocks, 1), lambda q, j: (0, 0)),
            pl.BlockSpec((slabs, rows), lambda q, j: (0, 0)),
            pl.BlockSpec((halves, 1, cap, sub * LANES), lambda q, j: (0, q, 0, j)),
            pl.BlockSpec((sub, slabs, rows), spot(first)),
        ]
        if sigma is not None:
            operands.append(sigma)
            specs.append(pl.BlockSpec(memory_space=pl.ANY))
        return pl.pallas_call(
            functools.partial(finish_kernel, tiles),
            grid=(parts, width),
            in_specs=specs,
            out_specs=pl.BlockSpec((sub, slabs, rows), spot(first)),
            out_shape=jax.ShapeDtypeStruct((feature, slabs, rows), jnp.bfloat16),
            input_output_aliases={} if sigma is None else {4: 0},
            compiler_params=params,
            cost_estimate=pl.CostEstimate(
                flops=2 * parts * width * sub * cap * blocks * span,
                bytes_accessed=parts * width * sub * (6 * slabs * rows + 2 * cap * span),
                transcendentals=0,
            ),
            name="finish",
        )(*operands)

    full_table = lax.all_gather(left_doubles, "grp", axis=1, tiled=True)
    picked = jnp.take(full_table, pair_index, axis=1).astype(jnp.float32)
    occ_hot = (
        jnp.arange(ov_block.shape[0], dtype=jnp.int32)[:, None] == occ_index[None, :]
    ).astype(jnp.bfloat16)
    occ_rows = lax.dot_general(
        ov_block, occ_hot, (((0,), (0,)), ((), ())), preferred_element_type=jnp.float32
    )
    vv_turned = vv_block.T
    pieces = 1
    piece = tiles // pieces

    swaps = [
        (axis, 1 << bit)
        for axis in ("grp", "tile")
        for bit in range((lax.axis_size(axis) - 1).bit_length())
    ]
    swaps = [swap for swap in swaps if swap != ("tile", 1)]
    early = sum(axis == "grp" for axis, _ in swaps)

    def add_swapped(x, steps):
        for axis, bit in steps:
            x = x + lax.ppermute(x, axis, [(k, k ^ bit) for k in range(lax.axis_size(axis))])
        return x

    half_rows = -(-feature // 16) * 8
    odd = lax.axis_index("tile") % 2 == 1

    def to_twin(x):
        return lax.ppermute(x, "tile", [(k, k ^ 1) for k in range(count)])

    def halve(x):
        top, bottom = x[:half_rows], x[feature - half_rows :]
        return jnp.where(odd, bottom, top) + to_twin(jnp.where(odd, top, bottom))

    def rejoin(x):
        other = to_twin(x)
        top, bottom = jnp.where(odd, other, x), jnp.where(odd, x, other)
        return jnp.concatenate([top, bottom[2 * half_rows - feature :]], axis=0)

    count_chunks = len(chunks)
    dens = jnp.zeros((feature, feature), jnp.float32)
    local = None
    begun = 0
    sent = []
    packed = pack(chunks[0], place)
    for i in range(count_chunks):
        gates = [sent[-1]] if sent else []
        if local is not None:
            gates = gates + [dens]
        sent.append(exchange(after(packed, *gates)))
        if i + 1 < count_chunks:
            packed = pack(chunks[i + 1], after(place, *gates))
        if i >= 1 and begun < pieces:
            local, dens = local_terms(
                (begun * piece, piece), after(live.T, packed), left, right, vv_turned, picked,
                occ_rows, dens, local,
            )
            begun += 1
            if begun == pieces:
                dens = halve(add_swapped(dens, swaps[:early]))
    while begun < pieces:
        local, dens = local_terms(
            (begun * piece, piece), live.T, left, right, vv_turned, picked, occ_rows, dens, local
        )
        begun += 1
    if count_chunks < 2:
        dens = halve(add_swapped(dens, swaps[:early]))
    norm_scale = math.sqrt(slabs * count * rows * lax.axis_size("grp"))
    dens = add_swapped(after(dens, *sent[:-1]), swaps[early:-1])

    entry = jnp.arange(blocks, dtype=jnp.int32)
    hit = tables[:, None, :] == jnp.arange(cap, dtype=jnp.int32)[None, :, None]
    index = jnp.sum(jnp.where(hit, entry[None, None, :] + 1, 0), axis=2) - 1
    owner = jnp.arange(count, dtype=jnp.int32)[:, None]
    slab_of = jnp.where(index >= 0, index % slabs + owner * slabs, -1).reshape(-1)
    tile_of = (index // slabs).reshape(-1)
    onehot = (
        slab_of[:, None] == jnp.arange(slab_block.shape[0], dtype=jnp.int32)[None, :]
    ).astype(jnp.bfloat16)
    picked_rows = jnp.dot(onehot, slab_block, preferred_element_type=jnp.float32).astype(jnp.bfloat16)
    weights = lax.dot_general(
        picked_rows, onehot, (((1,), (1,)), ((), ())), preferred_element_type=jnp.float32
    )
    weights = jnp.where(tile_of[:, None] == tile_of[None, :], weights, 0.0).astype(jnp.bfloat16)

    alive = jnp.repeat(live.astype(jnp.float32), span, axis=1)
    sigma = None
    backs = []
    for i in range(count_chunks):
        mixed = mix(chunks[i], weights, sent[i])
        gates = [backs[-1]] if i >= 1 else [sent[-1]]
        if i == 0:
            gates.append(dens)
            dens = add_swapped(after(dens, sent[-1]), swaps[early:][-1:])
        elif i == 1:
            gates.append(dens)
            density = rejoin(after(dens, backs[0])) / norm_scale
        elif i == count_chunks - 1:
            gates.append(density)
        if i >= 2:
            sigma = finish(chunks[i - 2], backs[i - 2], local, sigma)
            mixed, sigma = lax.optimization_barrier((mixed, sigma) + tuple(gates))[:2]
        else:
            mixed = after(mixed, *gates)
        backs.append(exchange(mixed))
    if count_chunks == 1:
        density = rejoin(dens) / norm_scale
    for i in range(max(0, count_chunks - 2), count_chunks):
        back = backs[i]
        if i == count_chunks - 1:
            back, density = lax.optimization_barrier((back, density))
        sigma = finish(chunks[i], back, local, sigma)
    return sigma, density


def caps_of(blocks):
    marks = [80, 88, 96, 104, 112, 128]
    return [m for m in marks if m < blocks] + [-(-blocks // 16) * 16]


def body(
    left_triples,
    right_triples,
    live_tiles,
    vv_block,
    slab_block,
    left_doubles,
    ov_block,
    pair_index,
    occ_index,
):
    slabs, rows, feature = left_triples.shape
    tiles = live_tiles.shape[1]
    count = lax.axis_size("tile")
    sizes = (feature, slabs, rows, tiles, count)
    left = jnp.transpose(left_triples, (2, 0, 1))
    right = jnp.transpose(right_triples, (2, 0, 1))

    own = live_tiles.T.reshape(-1)
    place = jnp.where(own > 0, jnp.cumsum(own) - 1, -1)
    devices = count * lax.axis_size("grp")
    everyone = lax.all_to_all(
        jnp.broadcast_to(place, (devices, 1, tiles * slabs)), ("tile", "grp"), 0, 0, tiled=True
    )
    most = jnp.max(everyone) + 1
    tables = lax.dynamic_index_in_dim(
        everyone.reshape(count, -1, tiles * slabs), lax.axis_index("grp"), 1, keepdims=False
    )

    caps = caps_of(tiles * slabs)
    which = jnp.sum((most > jnp.array(caps[:-1], jnp.int32)).astype(jnp.int32))
    sigma, density = lax.switch(
        which,
        [functools.partial(packed_plan, cap, sizes) for cap in caps],
        left, right, live_tiles, place, tables, vv_block, slab_block, left_doubles,
        ov_block, pair_index, occ_index,
    )
    return jnp.transpose(sigma, (1, 2, 0)), density


def takes_packed(mesh, shape, tiles):
    slabs, rows = shape[0] // mesh.shape["tile"], shape[1] // mesh.shape["grp"]
    local_tiles = tiles // mesh.shape["grp"]
    span = rows // local_tiles
    return slabs % 16 == 0 and span % LANES == 0 and mesh.shape["tile"] % (span // LANES) == 0


def solution(mesh):
    in_specs = (
        P("tile", "grp", None),
        P("tile", "grp", None),
        P("tile", "grp"),
        P(),
        P(),
        P("tile", "grp"),
        P(),
        P("grp"),
        P("grp"),
    )
    out_specs = (P("tile", "grp", None), P())

    def program(left_triples, right_triples, live_tiles, *others):
        packed = takes_packed(mesh, left_triples.shape, live_tiles.shape[1])
        mapped = jax.shard_map(
            body if packed else plain_body,
            mesh=mesh,
            in_specs=in_specs,
            out_specs=out_specs,
            check_vma=False,
        )
        return mapped(left_triples, right_triples, live_tiles, *others)

    return program
```
